32 devices in a mesh: emit: 4 (over z), elem: 8 (over y, x, core).
Axes of the slice: x: 2, y: 2, z: 4, core: 2. Of those that a mesh axis runs over, the one named last changes fastest.
Arguments:
- traces: float32 [256, 1024, 1024], P('emit', 'elem'), may hold values from -6 to 6
- codes: float32 [4, 2, 128], replicated, may hold values from -0.5 to 0.5
- code_of: int32 [256], replicated, may hold values from 0 to 3
- order: int32 [256], replicated, may hold values from 0 to 255, each once
- steer: float32 [256, 1024, 256], P(None, 'elem'), may hold values from -0.1875 to 0.1875
Outputs:
- beams: float32 [256, 256, 256], P('elem', 'emit')
The draws below stay inside these ranges and needn't reach their ends.
Inputs may be any that keep to these rules, and one draw needn't show every extreme that they name: `order`: each value 0 to 255 appears exactly once.
All inputs are finite; a program needn't handle non-finite values.
Results may differ from the reference program's by a relative error of at most 0.000071.
Values sent between devices are 32-bit elements; how exact they have to be, the bound alone decides.
No kernel may reach another device: no remote copies, remote signals or barrier semaphores. Data moves between devices by JAX's collectives and lax.ppermute only.
A program may use at most 320 MiB of HBM per device.

```python
import jax
import jax.numpy as jnp
from jax import lax

E = 256
M = 1024
S = 1024
TAPS = 128
NB = 256
L = 128
NCODE = 4


def place_ends(result, own_key, low, top_value):
    shape = result.shape
    index_at = [jax.random.randint(jax.random.fold_in(own_key, axis), (), 0, shape[axis]) for axis in range(len(shape))]
    result = result.at[tuple(index_at)].set(low)
    longest = shape.index(max(shape))
    index_at[longest] = (index_at[longest] + 1) % shape[longest]
    return result.at[tuple(index_at)].set(top_value)


def raised(drawn, own_key, source, target, shards_of, factor):
    def block_of(dim):
        return (jnp.arange(drawn.shape[dim]) // (drawn.shape[dim] // shards_of)).reshape((-1,) + (1,) * (drawn.ndim - 1 - dim))

    first = jax.random.permutation(own_key, shards_of)[block_of(target)]
    second = (block_of(target) + shards_of // 2) % shards_of
    return jnp.where((block_of(source) == first) | (block_of(source) == second), factor * drawn, drawn)


def level_of(key, extent, pieces, low, high):
    level, own = 1.0, jax.random.fold_in(key, 6)
    for dim, shards_of in pieces:
        steps = jnp.exp(jax.random.uniform(jax.random.fold_in(own, dim), (shards_of,), jnp.float32, low / len(pieces), high / len(pieces)))
        level = level * jnp.repeat(steps, extent[dim] // shards_of).reshape([-1 if axis == dim else 1 for axis in range(len(extent))])
    return level


def centred(rng, shape, deviation, bound, pieces=(), held_as=jnp.bfloat16):
    entries = deviation * jax.random.normal(rng, shape, jnp.float32)
    if pieces:
        entries = entries * level_of(rng, shape, pieces, -0.22, 0.18)
    return jnp.clip(entries, -bound, bound).astype(held_as)


def noise_with(stream_key, extent, scale, bound, pieces, heavy, kind=jnp.bfloat16):
    values = scale * jax.random.normal(stream_key, extent, jnp.float32)
    if pieces:
        values = values * level_of(stream_key, extent, pieces, -0.22, 0.18)
    return jnp.clip(raised(values, jax.random.fold_in(stream_key, 3), *heavy), -bound, bound).astype(kind)


def setup_inputs(seed: int = 0) -> dict:
    key_of = jax.random.split(jax.random.key(seed), 6)
    return {
        "traces": centred(key_of[0], (E, M, S), 1.0, 6.0, ((0, 4), (1, 8)), jnp.float32),
        "codes": centred(key_of[1], (NCODE, 2, TAPS), TAPS ** -0.5, 0.5, (), jnp.float32),
        "code_of": place_ends(jax.random.randint(key_of[2], (E,), 0, NCODE), jax.random.fold_in(key_of[2], 1), 0, NCODE - 1).astype(jnp.int32),
        "order": jax.random.permutation(key_of[3], E).astype(jnp.int32),
        "steer": noise_with(key_of[4], (NB, M, 2 * L), (2 * M) ** -0.5, 0.1875, ((1, 8),), (1, 0, 8, 2.0), jnp.float32),
    }


def toeplitz_table(codes):
    taps = codes.shape[2]
    rows = jnp.arange(2 * taps, dtype=jnp.int32)[:, None]
    cols = jnp.arange(taps, dtype=jnp.int32)[None, :]
    offset = rows - cols
    inside = (offset >= 0) & (offset < taps)
    clipped = jnp.clip(offset, 0, taps - 1)
    in_phase = jnp.where(inside[None], codes[:, 0, :][:, clipped], 0.0)
    quadrature = jnp.where(inside[None], codes[:, 1, :][:, clipped], 0.0)
    return jnp.concatenate([in_phase, quadrature], axis=2).astype(jnp.float32)

def hadamard_signs(order, columns, emissions):
    parity = jnp.zeros((order.shape[0], columns.shape[0]), jnp.int32)
    for bit in range(emissions.bit_length()):
        parity = parity + (order[:, None] >> bit & columns[None, :] >> bit & 1)
    signs = (1 - 2 * (parity % 2)).astype(jnp.float32)
    return signs / jnp.sqrt(jnp.float32(emissions))

def reference(traces, codes, code_of, order, steer):
    table = toeplitz_table(codes)
    nblock = S // TAPS
    freqs = jnp.mod(jnp.arange(NB, dtype=jnp.int32) - NB // 2, S).astype(jnp.int32)

    def one_emission(args):
        trace, code_index = args
        padded = jnp.concatenate([trace, jnp.zeros((M, TAPS), trace.dtype)], axis=1).reshape(M, nblock + 1, TAPS)
        windows = jnp.concatenate([padded[:, :-1], padded[:, 1:]], axis=2)
        picked = table[code_index]
        corr = jnp.einsum('mnj,jd->mnd', windows, picked, precision=lax.Precision.HIGHEST)
        corr_i = corr[:, :, :TAPS].reshape(M, S)
        corr_q = corr[:, :, TAPS:].reshape(M, S)
        spectrum = jnp.fft.fft(corr_i + 1j * corr_q, axis=1)[:, freqs] / jnp.sqrt(jnp.float32(S))
        return jnp.concatenate([jnp.real(spectrum), jnp.imag(spectrum)], axis=1).astype(traces.dtype)
    spectra = lax.map(one_emission, (traces, code_of))
    hadamard = hadamard_signs(order, jnp.arange(E, dtype=jnp.int32), E)
    decoded = jnp.dot(hadamard.T, spectra.reshape(E, M * 2 * NB), precision=lax.Precision.HIGHEST).reshape(E, M, 2 * NB)
    real_part = decoded[:, :, :NB]
    imag_part = decoded[:, :, NB:]
    first = jnp.einsum('kmb,bml->bkl', real_part, steer, precision=lax.Precision.HIGHEST)
    second = jnp.einsum('kmb,bml->bkl', imag_part, steer, precision=lax.Precision.HIGHEST)
    return jnp.concatenate([first[..., :L] - second[..., L:], first[..., L:] + second[..., :L]], axis=2)
```

```python
import functools

import jax
import jax.numpy as jnp
import numpy as np
from jax import lax
from jax.experimental import pallas as pl
from jax.experimental.pallas import tpu as pltpu
from jax.sharding import PartitionSpec as P


ROWS = 8
VMEM_LIMIT = 56 * 1024 * 1024


def split(value):
    high = value.astype(jnp.bfloat16)
    low = (value - high.astype(jnp.float32)).astype(jnp.bfloat16)
    return high, low


def dot(left, right):
    return lax.dot_general(left, right, (((1,), (0,)), ((), ())), preferred_element_type=jnp.float32)


def phase_tables(samples, taps, freqs):
    inner = np.arange(taps)[:, None] * freqs[None, :] % samples * (2 * np.pi / samples)
    outer = np.arange(samples // taps)[:, None] * taps * freqs[None, :] % samples * (2 * np.pi / samples)
    return tuple(f(a).astype(np.float32) for a in (inner, outer) for f in (np.cos, np.sin))


def spectral_kernel(code_ref, x_ref, codes_ref, cos_ref, sin_ref, wcos_ref, wsin_ref, out_ref, high_ref, low_ref, *, scale):
    rows, mdev, samples = x_ref.shape
    ncode, taps, _ = codes_ref.shape
    nbin = cos_ref.shape[1]
    nblock = samples // taps
    step = pl.program_id(0)

    @pl.when(step == 0)
    def _():
        cosine, sine = cos_ref[...], sin_ref[...]
        row = lax.broadcasted_iota(jnp.int32, (taps, taps), 0)
        col = lax.broadcasted_iota(jnp.int32, (taps, taps), 1)
        triangle = jnp.where(col <= row, 1.0, 0.0).astype(jnp.float32)

        def build(code, carry):
            pair = codes_ref[code]
            ci = jnp.broadcast_to(pair[:, 0:1], (taps, nbin))
            cq = jnp.broadcast_to(pair[:, 1:2], (taps, nbin))
            real = ci * cosine - cq * sine
            imag = ci * sine + cq * cosine
            summed = lax.dot_general(
                triangle, jnp.concatenate([real, imag], axis=1), (((1,), (0,)), ((), ())),
                precision=lax.Precision.HIGHEST, preferred_element_type=jnp.float32,
            ) * scale
            pr, pi = summed[:, :nbin], summed[:, nbin:]

            def put(block, tr, ti):
                th, tl = split(jnp.concatenate([tr, ti], axis=1))
                high_ref[code, pl.ds(block * taps, taps), :] = th
                low_ref[code, pl.ds(block * taps, taps), :] = tl

            put(0, cosine * pr + sine * pi, cosine * pi - sine * pr)
            gr, gi = pr[taps - 1 :, :], pi[taps - 1 :, :]
            br, bi = cosine * gr + sine * gi, cosine * gi - sine * gr
            for block in range(1, nblock):
                wr, wi = wcos_ref[block : block + 1, :], wsin_ref[block : block + 1, :]
                put(block, br * wr + bi * wi, bi * wr - br * wi)
            return carry

        lax.fori_loop(0, ncode, build, 0)

    flat = out_ref.reshape(out_ref.shape[0] * rows, mdev)

    def emission(e, carry):
        code = code_ref[step * rows + e]
        xh, xl = split(x_ref[e])
        both = dot(jnp.concatenate([xh, xl], axis=0), high_ref[code])
        result = both[:mdev] + both[mdev:] + dot(xh, low_ref[code])
        flat[pl.ds(e, out_ref.shape[0], stride=rows), :] = result.T
        return carry

    lax.fori_loop(0, rows, emission, 0)


def spectra_of(traces, codes_t, own_codes, freqs, scale, bins):
    edev, mdev, samples = traces.shape
    ncode, taps, _ = codes_t.shape
    nbin = freqs.shape[0]
    tables = phase_tables(samples, taps, freqs)
    rows = ROWS

    def whole(shape):
        return pl.BlockSpec(shape, lambda i, c, n=len(shape): (0,) * n)

    return pl.pallas_call(
        functools.partial(spectral_kernel, scale=scale),
        grid_spec=pltpu.PrefetchScalarGridSpec(
            num_scalar_prefetch=1,
            grid=(edev // rows,),
            in_specs=[pl.BlockSpec((rows, mdev, samples), lambda i, c: (i, 0, 0)), whole(codes_t.shape)]
            + [whole(t.shape) for t in tables],
            out_specs=pl.BlockSpec((2 * nbin, rows, mdev), lambda i, c: (0, i, 0)),
            scratch_shapes=[pltpu.VMEM((ncode, samples, 2 * nbin), jnp.bfloat16)] * 2,
        ),
        out_shape=jax.ShapeDtypeStruct((2 * nbin, edev, mdev), jnp.float32),
        compiler_params=pltpu.CompilerParams(vmem_limit_bytes=VMEM_LIMIT),
        cost_estimate=pl.CostEstimate(
            flops=edev * mdev * samples * 2 * nbin * 6, bytes_accessed=traces.size * 4 + 2 * nbin * edev * mdev * 4, transcendentals=0
        ),
        name="spectral",
    )(own_codes, traces, codes_t, *[jnp.asarray(t) for t in tables])


def steer_kernel(target_ref, spectra_ref, steer_ref, *refs):
    added, out_ref = refs[:-1], refs[-1]
    nb, mdev, width = steer_ref.shape
    half = width // 2
    for i in range(nb):
        wh, wl = split(steer_ref[i])

        def complex_rows(w):
            return jnp.concatenate([w, jnp.concatenate([-w[:, half:], w[:, :half]], axis=1)], axis=0)

        source = jnp.concatenate([spectra_ref[0, i], spectra_ref[1, i]], axis=1)
        sh, sl = split(source)
        edev = source.shape[0]
        both = dot(jnp.concatenate([sh, sl], axis=0), complex_rows(wh))
        result = both[:edev] + both[edev:] + dot(sh, complex_rows(wl))
        for ref in added:
            result = result + ref[0, i]
        out_ref[0, i] = result


def steer_blocks(targets, spectra, steer, added, offsets, nb, group, groups, local, locals_):
    count = targets.shape[0]
    _, _, edev, mdev = spectra.shape
    width = steer.shape[2]
    return pl.pallas_call(
        steer_kernel,
        grid_spec=pltpu.PrefetchScalarGridSpec(
            num_scalar_prefetch=1,
            grid=(count,),
            in_specs=[
                pl.BlockSpec((2, nb, edev, mdev), lambda i, t: (0, t[i] * locals_ + local, 0, 0)),
                pl.BlockSpec((nb, mdev, width), lambda i, t: (t[i] * groups + group, 0, 0)),
            ]
            + [pl.BlockSpec((1, nb, edev, width), lambda i, t, o=o: (i + o, 0, 0, 0)) for o in offsets],
            out_specs=pl.BlockSpec((1, nb, edev, width), lambda i, t: (i, 0, 0, 0)),
        ),
        out_shape=jax.ShapeDtypeStruct((count, nb, edev, width), jnp.float32),
        compiler_params=pltpu.CompilerParams(vmem_limit_bytes=VMEM_LIMIT),
        cost_estimate=pl.CostEstimate(
            flops=count * nb * edev * 2 * mdev * width * 2 * 6,
            bytes_accessed=4 * count * nb * (2 * edev * mdev + mdev * width + edev * width * (1 + len(added))),
            transcendentals=0,
        ),
        name="steer",
    )(targets, spectra, steer, *added)


def decode_kernel(signs_ref, own_ref, near_ref, out_ref):
    nb = own_ref.shape[0]
    count, kdev, _ = signs_ref.shape
    signs = signs_ref[...].reshape(count * kdev, signs_ref.shape[2])
    for i in range(nb):
        high, low = split(jnp.concatenate([own_ref[i], near_ref[i]], axis=0))
        result = dot(signs, high) + dot(signs, low)
        for j in range(count):
            out_ref[j, i] = result[j * kdev : (j + 1) * kdev]


def decode(signs, own, near):
    nb, _, width = own.shape
    count, kdev, _ = signs.shape
    return pl.pallas_call(
        decode_kernel,
        out_shape=jax.ShapeDtypeStruct((count, nb, kdev, width), jnp.float32),
        compiler_params=pltpu.CompilerParams(vmem_limit_bytes=VMEM_LIMIT),
        cost_estimate=pl.CostEstimate(
            flops=signs.size * nb * width * 4, bytes_accessed=4 * (2 * own.size + count * nb * kdev * width), transcendentals=0
        ),
        name="decode",
    )(signs, own, near)


def finish_kernel(*refs, scale, held):
    parts, out_ref = refs[held : -1], refs[-1]
    total = parts[0][0]
    for part in parts[1:]:
        total = total + part[0]
    out_ref[...] = total * scale


def finish(beams, own, arrived, group, groups, scale):
    _, nb, kdev, width = own.shape
    block = pl.BlockSpec((1, nb, kdev, width), lambda i: (0, 0, 0, 0))
    held = [] if beams is None else [beams]
    return pl.pallas_call(
        functools.partial(finish_kernel, scale=scale, held=len(held)),
        grid=(1,),
        in_specs=[pl.BlockSpec(memory_space=pl.ANY)] * len(held) + [block] * (1 + len(arrived)),
        out_specs=pl.BlockSpec((nb, kdev, width), lambda i: (group, 0, 0)),
        out_shape=jax.ShapeDtypeStruct((nb * groups, kdev, width), jnp.float32),
        input_output_aliases={0: 0} if held else {},
        cost_estimate=pl.CostEstimate(flops=2 * nb * kdev * width, bytes_accessed=4 * (2 + len(arrived)) * nb * kdev * width, transcendentals=0),
        name="finish",
    )(*held, own, *arrived)


def per_device(traces, codes, code_of, order, steer):
    edev, mdev, samples = traces.shape
    taps = codes.shape[2]
    emissions = order.shape[0]
    bins = steer.shape[0]
    ne, nm = lax.axis_size("emit"), lax.axis_size("elem")
    bins_dev = bins // nm
    nb = 8
    groups = bins_dev // nb
    parts = 2
    locals_ = groups // parts
    me = lax.axis_index("elem")
    here = lax.axis_index("emit")
    own_codes = lax.dynamic_slice_in_dim(code_of, here * edev, edev)
    codes_t = jnp.transpose(codes, (0, 2, 1))

    nbit = nm.bit_length() - 1
    upper = list(range(1, nbit))
    orders = (upper, upper[::-1])
    nrel = 1 << (nbit - 1)

    def mask_of(core, rel):
        return sum((rel >> (nbit - 2 - s) & 1) << bit for s, bit in enumerate(orders[core]))

    masks = np.array([[mask_of(core, nrel - 1 - p) for p in range(nrel)] for core in (0, 1)], np.int32)
    core = me & 1
    mine = me ^ jnp.where(core == 0, masks[0], masks[1])
    theirs = me ^ 1 ^ jnp.where(core == 0, masks[1], masks[0])
    swaps = [[(i, i ^ 1) for i in range(nm)]]
    for s in range(nbit - 1):
        swaps.append([(i, i ^ (1 << orders[i & 1][s])) for i in range(nm)])

    near = here ^ 1
    rows = jnp.concatenate([lax.dynamic_slice_in_dim(order, z * edev, edev) for z in (here, near)])
    others = [2 * j for j in range(1, ne // 2)]
    wanted = jnp.stack([here ^ z for z in others + [0]])
    columns = wanted[:, None] * edev + jnp.arange(edev, dtype=jnp.int32)[None, :]
    parity = lax.population_count(columns[:, :, None] & rows[None, None, :]) & 1
    signs = (1 - 2 * parity).astype(jnp.bfloat16)

    scale = float(np.float32(1.0) / np.sqrt(np.float32(samples)))
    spectra = []
    for part in range(parts):
        held = np.arange(bins).reshape(nm, parts, -1)[:, part].reshape(-1)
        result = spectra_of(traces, codes_t, own_codes, held - bins // 2, scale, bins)
        spectra.append(result.reshape(2, held.shape[0], edev, mdev))

    beams = None
    for group in range(groups):
        part, local = divmod(group, locals_)
        call = functools.partial(
            steer_blocks, spectra=spectra[part], steer=steer, nb=nb, group=group, groups=groups, local=local, locals_=locals_
        )
        sent = call(theirs, added=[], offsets=[])
        arrived = [lax.ppermute(sent, "elem", swaps[0])]
        for s in range(1, nbit + 1):
            high = nrel >> (s - 1)
            low = high >> 1
            offsets = [(nrel >> k) - high for k in range(s)]
            out = call(mine[nrel - high : nrel - low], added=arrived, offsets=offsets)
            if s < nbit:
                arrived = arrived + [lax.ppermute(out, "elem", swaps[s])]
        own = out[0]
        other = lax.ppermute(own, "emit", [(z, z ^ 1) for z in range(ne)])
        partial = decode(signs, own, other)
        fetched = [
            lax.ppermute(partial[j : j + 1], "emit", [(z, z ^ gap) for z in range(ne)]) for j, gap in enumerate(others)
        ]
        beams = finish(
            beams, partial[len(others) :], fetched, group, groups, float(1.0 / np.sqrt(np.float32(emissions)))
        )
    return beams


def solution(mesh):
    placed = (P("emit", "elem", None), P(), P(), P(), P(None, "elem", None))
    return jax.shard_map(
        per_device, mesh=mesh, in_specs=placed, out_specs=P("elem", "emit", None), check_vma=False
    )
```

```python
import functools

import jax
import jax.numpy as jnp
import numpy as np
from jax import lax
from jax.experimental import pallas as pl
from jax.experimental.pallas import tpu as pltpu
from jax.sharding import PartitionSpec as P


ROWS = 8
VMEM_LIMIT = 24 * 1024 * 1024
ANY = pl.BlockSpec(memory_space=pl.ANY)


def split(value):
    high = value.astype(jnp.bfloat16)
    low = (value - high.astype(jnp.float32)).astype(jnp.bfloat16)
    return high, low


def dot(left, right):
    return lax.dot_general(left, right, (((1,), (0,)), ((), ())), preferred_element_type=jnp.float32)


def phase_table(samples, taps, freqs):
    freqs = np.concatenate([freqs, freqs])
    inner = np.arange(taps)[:, None] * freqs[None, :] % samples * (2 * np.pi / samples)
    outer = np.arange(samples // taps)[:, None] * taps * freqs[None, :] % samples * (2 * np.pi / samples)
    return np.concatenate([f(a).astype(np.float32) for a in (inner, outer) for f in (np.cos, np.sin)])


def folds(cls, nblock):
    half, quarter = nblock // 2, nblock // 4
    if cls % 2:
        return [([(1, half)], half)] + [([(1, j), (-1, j + half)], j) for j in range(1, half)]
    sign = 1 if cls == 0 else -1
    first = [(sign, quarter), (1, 2 * quarter), (sign, 3 * quarter)]
    return [(first, 0)] + [([(1, j)] + [(s, j + b) for s, b in first], j) for j in range(1, quarter)]


def spectral_kernel(base_ref, code_ref, x_ref, codes_hbm, table_hbm, *refs, scale, classes, tokens):
    count = len(classes)
    refs = refs[tokens:]
    outs, helds, (codes_ref, table_ref, sems) = refs[:count], refs[count : 2 * count], refs[2 * count :]
    rows, mdev, samples = x_ref.shape
    ncode, _, taps = codes_ref.shape
    nblock = samples // taps
    step = pl.program_id(0)

    @pl.when(step == 0)
    def _():
        copies = [pltpu.make_async_copy(codes_hbm, codes_ref, sems.at[0]), pltpu.make_async_copy(table_hbm, table_ref, sems.at[1])]
        for copy in copies:
            copy.start()
        for copy in copies:
            copy.wait()
        row = lax.broadcasted_iota(jnp.int32, (taps, taps), 0)
        col = lax.broadcasted_iota(jnp.int32, (taps, taps), 1)
        triangle = jnp.where(col <= row, 1.0, 0.0).astype(jnp.bfloat16)

        def build(code, carry):
            pair = codes_ref[code]
            ci, cq = (jnp.sum(jnp.where(row == col, pair[q : q + 1], 0.0), axis=1, keepdims=True) for q in (0, 1))
            for k, cls in enumerate(classes):
                cosine, sine = table_ref[k, :taps], table_ref[k, taps : 2 * taps]
                wcos_ref, wsin_ref = (table_ref.at[k, pl.ds(2 * taps + q * nblock, nblock)] for q in (0, 1))
                width = cosine.shape[1]
                left = lax.broadcasted_iota(jnp.int32, (taps, width), 1) < width // 2
                terms = split(jnp.concatenate([ci * cosine - cq * sine, ci * sine + cq * cosine], axis=1))
                summed = (dot(triangle, terms[0]) + dot(triangle, terms[1])) * scale
                pr, pi = summed[:, :width], summed[:, width:]
                sums = folds(cls, nblock)
                depth = (1 + len(sums)) * taps

                def put(place, value):
                    high, low = split(value)
                    both = jnp.concatenate([high, low], axis=1)
                    helds[k][code, pl.ds(place * taps, taps), :] = both
                    helds[k][code, pl.ds(depth + place * taps, taps), :] = both

                put(0, jnp.where(left, cosine * pr + sine * pi, cosine * pi - sine * pr))
                gr, gi = pr[taps - 1 :, :], pi[taps - 1 :, :]
                br, bi = cosine * gr + sine * gi, cosine * gi - sine * gr
                for place, (_, power) in enumerate(sums):
                    wr, wi = wcos_ref[power : power + 1, :], wsin_ref[power : power + 1, :]
                    put(1 + place, jnp.where(left, br * wr + bi * wi, bi * wr - br * wi))
            return carry

        lax.fori_loop(0, ncode, build, 0)

    for e in range(rows):
        code = code_ref[base_ref[0] + step * rows + e]
        for k, cls in enumerate(classes):
            parts = [x_ref[e, :, :taps]]
            for terms, _ in folds(cls, nblock):
                total = None
                for sign, b in terms:
                    block = x_ref[e, :, b * taps : (b + 1) * taps]
                    if total is None:
                        total = block if sign > 0 else -block
                    else:
                        total = total + block if sign > 0 else total - block
                parts.append(total)
            pairs = [split(p) for p in parts]
            source = jnp.concatenate([h for h, _ in pairs] + [l for _, l in pairs], axis=1)
            both = dot(source, helds[k][code])
            width = both.shape[1] // 2
            flat = outs[k].reshape(width * rows, mdev)
            flat[pl.ds(e, width, stride=rows), :] = (both[:, :width] + both[:, width:]).T


def spectra_of(traces, codes, code_of, base, classes, bins, scale, after):
    edev, mdev, samples = traces.shape
    ncode, _, taps = codes.shape
    rows = ROWS
    table = jnp.asarray(np.stack([phase_table(samples, taps, np.arange(cls, bins, 4) - bins // 2) for cls in classes]))
    width = 2 * (bins // 4)

    hbm = pl.BlockSpec(memory_space=pltpu.HBM)
    depths = [2 * (1 + len(folds(cls, samples // taps))) * taps for cls in classes]
    return pl.pallas_call(
        functools.partial(spectral_kernel, scale=scale, classes=classes, tokens=len(after)),
        grid_spec=pltpu.PrefetchScalarGridSpec(
            num_scalar_prefetch=2,
            grid=(edev // rows,),
            in_specs=[pl.BlockSpec((rows, mdev, samples), lambda i, *s: (i, 0, 0)), hbm, hbm] + [ANY] * len(after),
            out_specs=[pl.BlockSpec((width, rows, mdev), lambda i, *s: (0, i, 0))] * len(classes),
            scratch_shapes=[pltpu.VMEM((ncode, depth, 2 * width), jnp.bfloat16) for depth in depths]
            + [pltpu.VMEM(codes.shape, jnp.float32), pltpu.VMEM(table.shape, jnp.float32), pltpu.SemaphoreType.DMA((2,))],
        ),
        out_shape=[jax.ShapeDtypeStruct((width, edev, mdev), jnp.float32)] * len(classes),
        compiler_params=pltpu.CompilerParams(vmem_limit_bytes=VMEM_LIMIT),
        cost_estimate=pl.CostEstimate(
            flops=edev * mdev * sum(depths) * 2 * width * 2,
            bytes_accessed=traces.size * 4 + len(classes) * width * edev * mdev * 4, transcendentals=0,
        ),
        name="spectral",
    )(base, code_of, traces, codes, table, *after)


def steer_kernel(target_ref, *refs, tokens):
    spectra_refs, steer_refs = refs[:2], refs[2:4]
    sent_ref, kept_ref = refs[4 + tokens :]
    nb, _, width = steer_refs[0].shape
    half = width // 2
    step, steps = pl.program_id(0), pl.num_programs(0)

    def complex_rows(w):
        return jnp.concatenate([w, jnp.concatenate([-w[:, half:], w[:, :half]], axis=1)], axis=0)

    def compute(out_ref):
        for k in range(2):
            for i in range(nb):
                wh, wl = split(steer_refs[k][i])
                sh, sl = split(jnp.concatenate([spectra_refs[k][0, i], spectra_refs[k][1, i]], axis=1))
                edev = sh.shape[0]
                both = dot(jnp.concatenate([sh, sl], axis=0), complex_rows(wh))
                out_ref[k, i] = both[:edev] + both[edev:] + dot(sh, complex_rows(wl))

    @pl.when(step < steps // 2)
    def _():
        compute(sent_ref)

    @pl.when(step >= steps // 2)
    def _():
        compute(kept_ref)


def steer_blocks(targets, spectra, steer, cls, after):
    count = targets.shape[0] // 2
    _, total, edev, mdev = spectra.shape
    nb = total // (2 * count)
    width = steer.shape[3]
    edge = count // 2
    shape = jax.ShapeDtypeStruct((count, nb, edev, width), jnp.float32)
    return pl.pallas_call(
        functools.partial(steer_kernel, tokens=len(after)),
        grid_spec=pltpu.PrefetchScalarGridSpec(
            num_scalar_prefetch=1,
            grid=(count,),
            in_specs=[pl.BlockSpec((2, nb, edev, mdev), lambda i, t, k=k: (0, t[2 * i + k], 0, 0)) for k in range(2)]
            + [pl.BlockSpec((nb, None, mdev, width), lambda i, t, k=k: (t[2 * i + k], cls, 0, 0)) for k in range(2)]
            + [ANY] * len(after),
            out_specs=[
                pl.BlockSpec((2, nb, edev, width), lambda i, t: (jnp.minimum(i, edge - 1), 0, 0, 0)),
                pl.BlockSpec((2, nb, edev, width), lambda i, t: (jnp.maximum(i - edge, 0), 0, 0, 0)),
            ],
        ),
        out_shape=[shape, shape],
        compiler_params=pltpu.CompilerParams(vmem_limit_bytes=VMEM_LIMIT),
        cost_estimate=pl.CostEstimate(
            flops=total * edev * 2 * mdev * width * 2 * 3,
            bytes_accessed=4 * total * (2 * edev * mdev + mdev * width + edev * width), transcendentals=0,
        ),
        name="steer",
    )(targets, spectra, spectra, steer, steer, *after)


def decode_kernel(signs_ref, own_ref, near_ref, *refs, tokens):
    outs = refs[tokens:]
    nb = own_ref.shape[0]
    count, kdev, _ = signs_ref.shape
    signs = signs_ref[...].reshape(count * kdev, signs_ref.shape[2])
    for i in range(nb):
        high, low = split(jnp.concatenate([own_ref[i], near_ref[i]], axis=0))
        result = dot(signs, high) + dot(signs, low)
        for j in range(count):
            outs[j][i] = result[j * kdev : (j + 1) * kdev]


def decode(signs, own, near, after):
    nb, _, width = own.shape
    count, kdev, _ = signs.shape
    vmem = pl.BlockSpec(memory_space=pltpu.VMEM)
    return pl.pallas_call(
        functools.partial(decode_kernel, tokens=len(after)),
        in_specs=[vmem] * 3 + [ANY] * len(after),
        out_shape=[jax.ShapeDtypeStruct((nb, kdev, width), jnp.float32)] * count,
        compiler_params=pltpu.CompilerParams(vmem_limit_bytes=VMEM_LIMIT),
        cost_estimate=pl.CostEstimate(
            flops=signs.size * nb * width * 4, bytes_accessed=4 * (2 * own.size + count * nb * kdev * width), transcendentals=0
        ),
        name="decode",
    )(signs, own, near, *after)


def finish_kernel(*refs, scale, held):
    parts, out_ref = refs[held:-1], refs[-1]
    total = parts[0][...]
    for part in parts[1:]:
        total = total + part[...]
    out_ref[...] = total * scale


def finish(beams, own, arrived, cls, scale):
    nb, kdev, width = own.shape
    block = pl.BlockSpec((nb, kdev, width), lambda i: (0, 0, 0))
    held = [] if beams is None else [beams]
    return pl.pallas_call(
        functools.partial(finish_kernel, scale=scale, held=len(held)),
        grid=(1,),
        in_specs=[ANY] * len(held) + [block] * (1 + len(arrived)),
        out_specs=pl.BlockSpec((nb, None, kdev, width), lambda i: (0, cls, 0, 0)),
        out_shape=jax.ShapeDtypeStruct((nb, 4, kdev, width), jnp.float32),
        input_output_aliases={0: 0} if held else {},
        compiler_params=pltpu.CompilerParams(vmem_limit_bytes=VMEM_LIMIT),
        cost_estimate=pl.CostEstimate(
            flops=2 * nb * kdev * width, bytes_accessed=4 * (2 + len(arrived)) * nb * kdev * width, transcendentals=0
        ),
        name="finish",
    )(*held, own, *arrived)


def per_device(traces, codes, code_of, order, steer):
    edev, mdev, samples = traces.shape
    emissions = order.shape[0]
    bins = steer.shape[0]
    ne, nm = lax.axis_size("emit"), lax.axis_size("elem")
    me = lax.axis_index("elem")
    here = lax.axis_index("emit")
    base = (here * edev).reshape(1).astype(jnp.int32)
    steer = steer.reshape(bins // 4, 4, *steer.shape[1:])

    nbit = nm.bit_length() - 1
    upper = list(range(1, nbit))
    orders = (upper, upper[::-1])
    nrel = 1 << (nbit - 1)

    def mask_of(core, rel):
        return sum((rel >> (nbit - 2 - s) & 1) << bit for s, bit in enumerate(orders[core]))

    masks = np.array([[mask_of(core, nrel - 1 - p) for p in range(nrel)] for core in (0, 1)], np.int32)
    masks = np.stack([np.concatenate([1 ^ masks[1 - core], masks[core]]) for core in (0, 1)])
    targets = me ^ jnp.where(me & 1 == 0, masks[0], masks[1])
    swaps = [[(i, i ^ 1) for i in range(nm)]]
    for s in range(nbit - 1):
        swaps.append([(i, i ^ (1 << orders[i & 1][s])) for i in range(nm)])

    def signs_of(gap):
        rows = jnp.concatenate([lax.dynamic_slice_in_dim(order, z * edev, edev) for z in (here, here ^ gap)])
        others = others_of(gap, ne)
        wanted = jnp.stack([here ^ z for z in others + [0]])
        columns = wanted[:, None] * edev + jnp.arange(edev, dtype=jnp.int32)[None, :]
        parity = lax.population_count(columns[:, :, None] & rows[None, None, :]) & 1
        return others, (1 - 2 * parity).astype(jnp.bfloat16)

    scale = float(np.float32(1.0) / np.sqrt(np.float32(samples)))
    shrink = float(1.0 / np.sqrt(np.float32(emissions)))
    gaps = {cls: gap_of(cls, ne) for cls in range(4)}
    signs = {gap: signs_of(gap) for gap in sorted(set(gaps.values()))}

    last = []
    state = {cls: {} for cls in range(4)}
    beams = None

    def spectral(*classes):
        nonlocal last
        out = spectra_of(traces, codes, code_of, base, classes, bins, scale, last)
        for cls, spectra in zip(classes, out):
            state[cls]["spectra"] = spectra.reshape(2, bins // 4, edev, mdev)
        last = [out[0]]

    def steered(cls):
        nonlocal last
        sent, kept = steer_blocks(targets, state[cls]["spectra"], steer, cls, last)
        last = [sent]
        state[cls]["kept"] = kept
        state[cls]["arrived"] = [lax.ppermute(sent, "elem", swaps[0])]

    def added(cls):
        nonlocal last
        kept, arrived = state[cls]["kept"], state[cls]["arrived"]
        stage = len(arrived)
        high = nrel >> (stage - 1)
        low = high >> 1
        kept, _ = lax.optimization_barrier((kept, last[0]))
        total = kept[nrel - high : nrel - low]
        for k, array in enumerate(arrived):
            start = (nrel >> k) - high
            total = total + array[start : start + high - low]
        last = [total]
        if stage < nbit:
            arrived.append(lax.ppermute(total, "elem", swaps[stage]))
        else:
            own = total[0]
            state[cls]["own"] = own
            state[cls]["near"] = lax.ppermute(own, "emit", [(z, z ^ gaps[cls]) for z in range(ne)])

    def decoded(cls):
        nonlocal last
        others, held = signs[gaps[cls]]
        out = decode(held, state[cls]["own"], state[cls]["near"], last)
        last = [out[0]]
        state[cls]["partial"] = out[-1]
        state[cls]["fetched"] = [
            lax.ppermute(part, "emit", [(z, z ^ gap) for z in range(ne)]) for part, gap in zip(out, others)
        ]

    def finished(cls):
        nonlocal beams
        beams = finish(beams, state[cls]["partial"], state[cls]["fetched"], cls, shrink)

    steps = {"spectral": spectral, "steer": steered, "sum": added, "decode": decoded, "finish": finished}
    for name, *values in plan(nbit):
        steps[name](*values)
    return beams.reshape(-1, *beams.shape[2:])


def plan(nbit):
    more = range(nbit - 2)
    return [
        ("spectral", 2, 0), ("steer", 2), ("steer", 0), ("sum", 2),
        ("spectral", 1), *(("sum", 2) for _ in more), ("sum", 0), ("steer", 1), ("sum", 2),
        ("spectral", 3), *(("sum", 0) for _ in more), ("sum", 1), ("steer", 3), ("sum", 0),
        ("decode", 2), ("sum", 3), *(("sum", 1) for _ in more), ("sum", 1), *(("sum", 3) for _ in more),
        ("decode", 0), ("decode", 1), ("sum", 3), ("decode", 3),
        ("finish", 2), ("finish", 0), ("finish", 1), ("finish", 3),
    ]


def gap_of(cls, ne):
    return ne // 2 if cls in (2, 0) else 1


def others_of(gap, ne):
    return [z for z in range(1, ne) if not z & gap]


def solution(mesh):
    placed = (P("emit", "elem", None), P(), P(), P(), P(None, "elem", None))

    return jax.shard_map(per_device, mesh=mesh, in_specs=placed, out_specs=P("elem", "emit", None), check_vma=False)
```

```python
import functools

import jax
import jax.numpy as jnp
import numpy as np
from jax import lax
from jax.experimental import pallas as pl
from jax.experimental.pallas import tpu as pltpu
from jax.sharding import PartitionSpec as P


ROWS = 8
SLOTS = 3
VMEM_LIMIT = 24 * 1024 * 1024
ANY = pl.BlockSpec(memory_space=pl.ANY)


def split(value):
    high = value.astype(jnp.bfloat16)
    low = (value - high.astype(jnp.float32)).astype(jnp.bfloat16)
    return high, low


def dot(left, right):
    return lax.dot_general(left, right, (((1,), (0,)), ((), ())), preferred_element_type=jnp.float32)


def phase_table(samples, taps, freqs):
    inner = np.arange(taps)[:, None] * freqs[None, :] % samples * (2 * np.pi / samples)
    outer = np.arange(samples // taps)[:, None] * taps * freqs[None, :] % samples * (2 * np.pi / samples)
    cosine, sine, wcos, wsin = np.cos(inner), np.sin(inner), np.cos(outer), np.sin(outer)
    pairs = [(cosine, sine), (-sine, cosine), (cosine, cosine), (sine, sine), (wcos, wcos), (wsin, wsin)]
    return np.concatenate([np.concatenate(pair, axis=1) for pair in pairs]).astype(np.float32)


def folds(cls, nblock):
    half, quarter = nblock // 2, nblock // 4
    if cls % 2:
        return [([(1, half)], half)] + [([(1, j), (-1, j + half)], j) for j in range(1, half)]
    sign = 1 if cls == 0 else -1
    first = [(sign, quarter), (1, 2 * quarter), (sign, 3 * quarter)]
    return [(first, 0)] + [([(1, j)] + [(s, j + b) for s, b in first], j) for j in range(1, quarter)]


def spectral_kernel(base_ref, code_ref, codes_ref, table_ref, x_hbm, *refs, scale, classes, tokens):
    count = len(classes)
    refs = refs[tokens:]
    outs, helds, (x_ref, sems) = refs[:count], refs[count : 2 * count], refs[2 * count :]
    slots, rows, mdev, samples = x_ref.shape
    ncode, _, taps = codes_ref.shape
    nblock = samples // taps
    edev = x_hbm.shape[0]
    steps = edev // rows

    def fetch(step, slot):
        return pltpu.make_async_copy(x_hbm.at[pl.ds(step * rows, rows)], x_ref.at[slot], sems.at[slot])

    for step in range(min(slots, steps)):
        fetch(step, step).start()

    def tables():
        row = lax.broadcasted_iota(jnp.int32, (taps, taps), 0)
        col = lax.broadcasted_iota(jnp.int32, (taps, taps), 1)
        triangle = jnp.where(col <= row, 1.0, 0.0).astype(jnp.bfloat16)

        def build(code, carry):
            pair = codes_ref[code]
            ci, cq = (jnp.sum(jnp.where(row == col, pair[q : q + 1], 0.0), axis=1, keepdims=True) for q in (0, 1))
            for k, cls in enumerate(classes):
                first, second, cosine, sine = (table_ref[k, q * taps : (q + 1) * taps] for q in range(4))
                wcos_ref, wsin_ref = (table_ref.at[k, pl.ds(4 * taps + q * nblock, nblock)] for q in (0, 1))
                width = cosine.shape[1]
                left = lax.broadcasted_iota(jnp.int32, (taps, width), 1) < width // 2
                high, low = split(ci * first + cq * second)
                summed = (dot(triangle, high) + dot(triangle, low)) * scale
                turned = pltpu.roll(summed, width // 2, axis=1)
                turned = jnp.where(left, turned, -turned)
                sums = folds(cls, nblock)
                lead = (1 + len(sums)) // 2 * 2

                def put(place, value):
                    both = jnp.concatenate(split(value), axis=1)
                    helds[k][code, pl.ds(place * taps, taps), :] = both
                    if place == lead:
                        helds[k][code, pl.ds((place + 1) * taps, taps), :] = both

                put(0, cosine * summed + sine * turned)
                end, turned_end = summed[taps - 1 :, :], turned[taps - 1 :, :]
                whole, turned_whole = cosine * end + sine * turned_end, cosine * turned_end - sine * end
                for place, (_, power) in enumerate(sums):
                    put(1 + place, whole * wcos_ref[power : power + 1, :] + turned_whole * wsin_ref[power : power + 1, :])
            return carry

        lax.fori_loop(0, ncode, build, 0)

    def emission(step, slot, e):
        code = code_ref[base_ref[0] + step * rows + e]
        for k, cls in enumerate(classes):
            parts = [x_ref[slot, e, :, :taps]]
            for terms, _ in folds(cls, nblock):
                total = None
                for sign, b in terms:
                    block = x_ref[slot, e, :, b * taps : (b + 1) * taps]
                    if total is None:
                        total = block if sign > 0 else -block
                    else:
                        total = total + block if sign > 0 else total - block
                parts.append(total)
            pairs = [split(p) for p in parts]
            lead = len(pairs) // 2 * 2
            width = outs[k].shape[1]
            source = jnp.concatenate(
                [jnp.concatenate([p[q] for p in pairs[:lead]], axis=1) for q in (0, 1)], axis=0
            )
            both = dot(source, helds[k][code, : lead * taps])
            both = both[:mdev] + both[mdev:]
            if lead < len(pairs):
                both = both + dot(jnp.concatenate(pairs[lead], axis=1), helds[k][code, lead * taps :])
            flat = outs[k].reshape(steps * width * rows, mdev)
            flat[pl.ds(step * (width * rows) + e, width, stride=rows), :] = (both[:, :width] + both[:, width:]).T

    def work(step, carry):
        slot = lax.rem(step, slots)
        fetch(step, slot).wait()
        for e in range(rows):
            emission(step, slot, e)

        @pl.when(step + slots < steps)
        def _():
            fetch(step + slots, slot).start()

        return carry

    tables()
    lax.fori_loop(0, steps, work, 0)


def spectra_of(traces, codes, code_of, base, classes, bins, scale, after):
    edev, mdev, samples = traces.shape
    ncode, _, taps = codes.shape
    rows = ROWS
    table = jnp.asarray(np.stack([phase_table(samples, taps, np.arange(cls, bins, 4) - bins // 2) for cls in classes]))
    width = 2 * (bins // 4)

    chunks = [1 + len(folds(cls, samples // taps)) for cls in classes]
    depths = [(n + n % 2) * taps for n in chunks]
    vmem, smem = pl.BlockSpec(memory_space=pltpu.VMEM), pl.BlockSpec(memory_space=pltpu.SMEM)
    return pl.pallas_call(
        functools.partial(spectral_kernel, scale=scale, classes=classes, tokens=len(after)),
        in_specs=[smem, smem, vmem, vmem, pl.BlockSpec(memory_space=pltpu.HBM)] + [ANY] * len(after),
        out_specs=[vmem] * len(classes),
        scratch_shapes=[pltpu.VMEM((ncode, depth, 2 * width), jnp.bfloat16) for depth in depths]
        + [pltpu.VMEM((SLOTS, rows, mdev, samples), jnp.float32), pltpu.SemaphoreType.DMA((SLOTS,))],
        out_shape=[jax.ShapeDtypeStruct((edev // rows, width, rows, mdev), jnp.float32)] * len(classes),
        compiler_params=pltpu.CompilerParams(vmem_limit_bytes=VMEM_LIMIT),
        cost_estimate=pl.CostEstimate(
            flops=edev * mdev * 2 * sum(depths) * 2 * width * 2,
            bytes_accessed=traces.size * 4 + len(classes) * width * edev * mdev * 4, transcendentals=0,
        ),
        name="spectral",
    )(base, code_of, codes, table, traces, *after)


def steer_kernel(target_ref, spectra_ref, steer_hbm, *refs, cls, tokens):
    sent_ref, kept_ref, steer_ref, sems = refs[tokens:]
    slots, nb, mdev, width = steer_ref.shape
    count, _, edev, _ = sent_ref.shape
    half = width // 2

    def fetch(place, slot):
        source = steer_hbm.at[pl.ds(target_ref[place] * nb, nb), cls]
        return pltpu.make_async_copy(source, steer_ref.at[slot], sems.at[slot])

    for place in range(min(slots, 2 * count)):
        fetch(place, place).start()

    def complex_rows(w):
        return jnp.concatenate([w, jnp.concatenate([-w[:, half:], w[:, :half]], axis=1)], axis=0)

    def run(out_ref, first):
        def body(block, carry):
            place = first + block
            slot = lax.rem(place, slots)
            fetch(place, slot).wait()
            start = target_ref[place] * nb
            for i in range(nb):
                wh, wl = split(steer_ref[slot, i])
                parts = [spectra_ref[:, q, start + i].reshape(edev, mdev) for q in (0, 1)]
                sh, sl = split(jnp.concatenate(parts, axis=1))
                both = dot(jnp.concatenate([sh, sl], axis=0), complex_rows(wh))
                out_ref[block, i] = both[:edev] + both[edev:] + dot(sh, complex_rows(wl))

            @pl.when(place + slots < 2 * count)
            def _():
                fetch(place + slots, slot).start()

            return carry

        lax.fori_loop(0, count, body, 0)

    run(sent_ref, 0)
    run(kept_ref, count)


def steer_blocks(targets, spectra, steer, cls, after):
    count = targets.shape[0] // 2
    _, _, total, _, mdev = spectra.shape
    edev = spectra.shape[0] * spectra.shape[3]
    nb = total // (2 * count)
    width = steer.shape[3]
    shape = jax.ShapeDtypeStruct((count, nb, edev, width), jnp.float32)
    vmem, smem = pl.BlockSpec(memory_space=pltpu.VMEM), pl.BlockSpec(memory_space=pltpu.SMEM)
    return pl.pallas_call(
        functools.partial(steer_kernel, cls=cls, tokens=len(after)),
        in_specs=[smem, vmem, pl.BlockSpec(memory_space=pltpu.HBM)] + [ANY] * len(after),
        out_specs=[vmem, vmem],
        scratch_shapes=[pltpu.VMEM((4, nb, mdev, width), jnp.float32), pltpu.SemaphoreType.DMA((4,))],
        out_shape=[shape, shape],
        compiler_params=pltpu.CompilerParams(vmem_limit_bytes=VMEM_LIMIT),
        cost_estimate=pl.CostEstimate(
            flops=total * edev * 2 * mdev * width * 2 * 3,
            bytes_accessed=4 * total * (2 * edev * mdev + mdev * width + edev * width), transcendentals=0,
        ),
        name="steer",
    )(targets, spectra, steer, *after)


def decode_kernel(signs_ref, own_ref, near_ref, *refs, tokens):
    outs = refs[tokens:]
    nb = own_ref.shape[0]
    count, kdev, _ = signs_ref.shape
    signs = signs_ref[...].reshape(count * kdev, signs_ref.shape[2])
    for i in range(nb):
        high, low = split(jnp.concatenate([own_ref[i], near_ref[i]], axis=0))
        result = dot(signs, high) + dot(signs, low)
        for j in range(count):
            outs[j][i] = result[j * kdev : (j + 1) * kdev]


def decode(signs, own, near, after):
    nb, _, width = own.shape
    count, kdev, _ = signs.shape
    vmem = pl.BlockSpec(memory_space=pltpu.VMEM)
    return pl.pallas_call(
        functools.partial(decode_kernel, tokens=len(after)),
        in_specs=[vmem] * 3 + [ANY] * len(after),
        out_shape=[jax.ShapeDtypeStruct((nb, kdev, width), jnp.float32)] * count,
        compiler_params=pltpu.CompilerParams(vmem_limit_bytes=VMEM_LIMIT),
        cost_estimate=pl.CostEstimate(
            flops=signs.size * nb * width * 4, bytes_accessed=4 * (2 * own.size + count * nb * kdev * width), transcendentals=0
        ),
        name="decode",
    )(signs, own, near, *after)


def finish_kernel(*refs, scale, held):
    parts, out_ref = refs[held:-1], refs[-1]
    total = parts[0][...]
    for part in parts[1:]:
        total = total + part[...]
    out_ref[...] = total * scale


def finish(beams, own, arrived, cls, scale):
    nb, kdev, width = own.shape
    block = pl.BlockSpec((nb, kdev, width), lambda i: (0, 0, 0))
    held = [] if beams is None else [beams]
    return pl.pallas_call(
        functools.partial(finish_kernel, scale=scale, held=len(held)),
        grid=(1,),
        in_specs=[ANY] * len(held) + [block] * (1 + len(arrived)),
        out_specs=pl.BlockSpec((nb, None, kdev, width), lambda i: (0, cls, 0, 0)),
        out_shape=jax.ShapeDtypeStruct((nb, 4, kdev, width), jnp.float32),
        input_output_aliases={0: 0} if held else {},
        compiler_params=pltpu.CompilerParams(vmem_limit_bytes=VMEM_LIMIT),
        cost_estimate=pl.CostEstimate(
            flops=2 * nb * kdev * width, bytes_accessed=4 * (2 + len(arrived)) * nb * kdev * width, transcendentals=0
        ),
        name="finish",
    )(*held, own, *arrived)


def per_device(traces, codes, code_of, order, steer):
    edev, mdev, samples = traces.shape
    emissions = order.shape[0]
    bins = steer.shape[0]
    ne, nm = lax.axis_size("emit"), lax.axis_size("elem")
    me = lax.axis_index("elem")
    here = lax.axis_index("emit")
    base = (here * edev).reshape(1).astype(jnp.int32)
    steer = steer.reshape(bins // 4, 4, *steer.shape[1:])

    nbit = nm.bit_length() - 1
    upper = list(range(1, nbit))
    orders = (upper, upper[::-1])
    nrel = 1 << (nbit - 1)

    def mask_of(core, rel):
        return sum((rel >> (nbit - 2 - s) & 1) << bit for s, bit in enumerate(orders[core]))

    masks = np.array([[mask_of(core, nrel - 1 - p) for p in range(nrel)] for core in (0, 1)], np.int32)
    masks = np.stack([np.concatenate([1 ^ masks[1 - core], masks[core]]) for core in (0, 1)])
    targets = me ^ jnp.where(me & 1 == 0, masks[0], masks[1])
    swaps = [[(i, i ^ 1) for i in range(nm)]]
    for s in range(nbit - 1):
        swaps.append([(i, i ^ (1 << orders[i & 1][s])) for i in range(nm)])

    def signs_of(gap):
        rows = jnp.concatenate([lax.dynamic_slice_in_dim(order, z * edev, edev) for z in (here, here ^ gap)])
        others = others_of(gap, ne)
        wanted = jnp.stack([here ^ z for z in others + [0]])
        columns = wanted[:, None] * edev + jnp.arange(edev, dtype=jnp.int32)[None, :]
        parity = lax.population_count(columns[:, :, None] & rows[None, None, :]) & 1
        return others, (1 - 2 * parity).astype(jnp.bfloat16)

    scale = float(np.float32(1.0) / np.sqrt(np.float32(samples)))
    shrink = float(1.0 / np.sqrt(np.float32(emissions)))
    gaps = {cls: gap_of(cls, ne) for cls in range(4)}
    signs = {gap: signs_of(gap) for gap in sorted(set(gaps.values()))}

    last = []
    state = {cls: {} for cls in range(4)}
    beams = None

    def spectral(*classes):
        nonlocal last
        out = spectra_of(traces, codes, code_of, base, classes, bins, scale, last)
        for cls, spectra in zip(classes, out):
            state[cls]["spectra"] = spectra.reshape(edev // ROWS, 2, bins // 4, ROWS, mdev)
        last = [out[0]]

    def steered(cls):
        nonlocal last
        sent, kept = steer_blocks(targets, state[cls]["spectra"], steer, cls, last)
        last = [sent]
        state[cls]["kept"] = kept
        state[cls]["arrived"] = [lax.ppermute(sent, "elem", swaps[0])]

    def added(cls):
        nonlocal last
        kept, arrived = state[cls]["kept"], state[cls]["arrived"]
        stage = len(arrived)
        high = nrel >> (stage - 1)
        low = high >> 1
        kept, _ = lax.optimization_barrier((kept, last[0]))
        total = kept[nrel - high : nrel - low]
        for k, array in enumerate(arrived):
            start = (nrel >> k) - high
            total = total + array[start : start + high - low]
        last = [total]
        if stage < nbit:
            arrived.append(lax.ppermute(total, "elem", swaps[stage]))
        else:
            own = total[0]
            state[cls]["own"] = own
            state[cls]["near"] = lax.ppermute(own, "emit", [(z, z ^ gaps[cls]) for z in range(ne)])

    def decoded(cls):
        nonlocal last
        others, held = signs[gaps[cls]]
        out = decode(held, state[cls]["own"], state[cls]["near"], last)
        last = [out[0]]
        state[cls]["partial"] = out[-1]
        state[cls]["fetched"] = [
            lax.ppermute(part, "emit", [(z, z ^ gap) for z in range(ne)]) for part, gap in zip(out, others)
        ]

    def finished(cls):
        nonlocal beams
        beams = finish(beams, state[cls]["partial"], state[cls]["fetched"], cls, shrink)

    steps = {"spectral": spectral, "steer": steered, "sum": added, "decode": decoded, "finish": finished}
    for name, *values in plan(nbit):
        steps[name](*values)
    return beams.reshape(-1, *beams.shape[2:])


def plan(nbit):
    more = range(nbit - 2)
    return [
        ("spectral", 2, 0), ("steer", 2), ("steer", 0), ("sum", 2),
        ("spectral", 1), *(("sum", 2) for _ in more), ("steer", 1), ("sum", 2), ("sum", 0),
        ("spectral", 3), *(("sum", 0) for _ in more), ("sum", 1), ("steer", 3), ("sum", 0),
        ("decode", 2), *(("sum", 1) for _ in more), ("sum", 3), ("sum", 1), *(("sum", 3) for _ in more), ("sum", 3),
        ("decode", 1), ("decode", 3), ("decode", 0),
        ("finish", 2), ("finish", 1), ("finish", 0), ("finish", 3),
    ]


def gap_of(cls, ne):
    return ne // 2 if cls in (2, 0) else 1


def others_of(gap, ne):
    return [z for z in range(1, ne) if not z & gap]


def solution(mesh):
    placed = (P("emit", "elem", None), P(), P(), P(), P(None, "elem", None))

    return jax.shard_map(per_device, mesh=mesh, in_specs=placed, out_specs=P("elem", "emit", None), check_vma=False)
```

```python
import functools

import jax
import jax.numpy as jnp
import numpy as np
from jax import lax
from jax.experimental import pallas as pl
from jax.experimental.pallas import tpu as pltpu
from jax.sharding import PartitionSpec as P


ROWS = 8
SLOTS = 3
VMEM_LIMIT = 24 * 1024 * 1024
STEER_VMEM_LIMIT = 32 * 1024 * 1024
ANY = pl.BlockSpec(memory_space=pl.ANY)


def split(value):
    high = value.astype(jnp.bfloat16)
    low = (value - high.astype(jnp.float32)).astype(jnp.bfloat16)
    return high, low


def dot(left, right):
    return lax.dot_general(left, right, (((1,), (0,)), ((), ())), preferred_element_type=jnp.float32)


def phase_table(samples, taps, freqs):
    inner = np.arange(taps)[:, None] * freqs[None, :] % samples * (2 * np.pi / samples)
    outer = np.arange(samples // taps)[:, None] * taps * freqs[None, :] % samples * (2 * np.pi / samples)
    cosine, sine, wcos, wsin = np.cos(inner), np.sin(inner), np.cos(outer), np.sin(outer)
    pairs = [(cosine, sine), (-sine, cosine), (cosine, cosine), (sine, sine), (wcos, wcos), (wsin, wsin)]
    return np.concatenate([np.concatenate(pair, axis=1) for pair in pairs]).astype(np.float32)


def folds(cls, nblock):
    half, quarter = nblock // 2, nblock // 4
    if cls % 2:
        return [([(1, half)], half)] + [([(1, j), (-1, j + half)], j) for j in range(1, half)]
    sign = 1 if cls == 0 else -1
    first = [(sign, quarter), (1, 2 * quarter), (sign, 3 * quarter)]
    return [(first, 0)] + [([(1, j)] + [(s, j + b) for s, b in first], j) for j in range(1, quarter)]


def spectral_kernel(base_ref, code_ref, codes_ref, table_ref, x_hbm, *refs, scale, classes, tokens):
    count = len(classes)
    refs = refs[tokens:]
    outs, helds, (x_ref, sems) = refs[:count], refs[count : 2 * count], refs[2 * count :]
    slots, rows, mdev, samples = x_ref.shape
    ncode, _, taps = codes_ref.shape
    nblock = samples // taps
    edev = x_hbm.shape[0]
    steps = edev // rows

    def fetch(step, slot):
        return pltpu.make_async_copy(x_hbm.at[pl.ds(step * rows, rows)], x_ref.at[slot], sems.at[slot])

    for step in range(min(slots, steps)):
        fetch(step, step).start()

    def tables():
        row = lax.broadcasted_iota(jnp.int32, (taps, taps), 0)
        col = lax.broadcasted_iota(jnp.int32, (taps, taps), 1)
        triangle = jnp.where(col <= row, 1.0, 0.0).astype(jnp.bfloat16)

        def build(code, carry):
            pair = codes_ref[code]
            ci, cq = (jnp.sum(jnp.where(row == col, pair[q : q + 1], 0.0), axis=1, keepdims=True) for q in (0, 1))
            for k, cls in enumerate(classes):
                first, second, cosine, sine = (table_ref[k, q * taps : (q + 1) * taps] for q in range(4))
                wcos_ref, wsin_ref = (table_ref.at[k, pl.ds(4 * taps + q * nblock, nblock)] for q in (0, 1))
                width = cosine.shape[1]
                left = lax.broadcasted_iota(jnp.int32, (taps, width), 1) < width // 2
                high, low = split(ci * first + cq * second)
                summed = (dot(triangle, high) + dot(triangle, low)) * scale
                turned = pltpu.roll(summed, width // 2, axis=1)
                turned = jnp.where(left, turned, -turned)
                sums = folds(cls, nblock)
                lead = (1 + len(sums)) // 2 * 2

                def put(place, value):
                    both = jnp.concatenate(split(value), axis=1)
                    helds[k][code, pl.ds(place * taps, taps), :] = both
                    if place == lead:
                        helds[k][code, pl.ds((place + 1) * taps, taps), :] = both

                put(0, cosine * summed + sine * turned)
                end, turned_end = summed[taps - 1 :, :], turned[taps - 1 :, :]
                whole, turned_whole = cosine * end + sine * turned_end, cosine * turned_end - sine * end
                for place, (_, power) in enumerate(sums):
                    put(1 + place, whole * wcos_ref[power : power + 1, :] + turned_whole * wsin_ref[power : power + 1, :])
            return carry

        lax.fori_loop(0, ncode, build, 0)

    def emission(step, slot, e):
        code = code_ref[base_ref[0] + step * rows + e]
        for k, cls in enumerate(classes):
            parts = [x_ref[slot, e, :, :taps]]
            for terms, _ in folds(cls, nblock):
                total = None
                for sign, b in terms:
                    block = x_ref[slot, e, :, b * taps : (b + 1) * taps]
                    if total is None:
                        total = block if sign > 0 else -block
                    else:
                        total = total + block if sign > 0 else total - block
                parts.append(total)
            pairs = [split(p) for p in parts]
            lead = len(pairs) // 2 * 2
            width = outs[k].shape[1]
            source = jnp.concatenate(
                [jnp.concatenate([p[q] for p in pairs[:lead]], axis=1) for q in (0, 1)], axis=0
            )
            both = dot(source, helds[k][code, : lead * taps])
            both = both[:mdev] + both[mdev:]
            if lead < len(pairs):
                both = both + dot(jnp.concatenate(pairs[lead], axis=1), helds[k][code, lead * taps :])
            flat = outs[k].reshape(steps * width * rows, mdev)
            flat[pl.ds(step * (width * rows) + e, width, stride=rows), :] = (both[:, :width] + both[:, width:]).T

    def work(step, carry):
        slot = lax.rem(step, slots)
        fetch(step, slot).wait()
        for e in range(rows):
            emission(step, slot, e)

        @pl.when(step + slots < steps)
        def _():
            fetch(step + slots, slot).start()

        return carry

    tables()
    lax.fori_loop(0, steps, work, 0)


def spectra_of(traces, codes, code_of, base, classes, bins, scale, after):
    edev, mdev, samples = traces.shape
    ncode, _, taps = codes.shape
    rows = ROWS
    table = jnp.asarray(np.stack([phase_table(samples, taps, np.arange(cls, bins, 4) - bins // 2) for cls in classes]))
    width = 2 * (bins // 4)

    chunks = [1 + len(folds(cls, samples // taps)) for cls in classes]
    depths = [(n + n % 2) * taps for n in chunks]
    vmem, smem = pl.BlockSpec(memory_space=pltpu.VMEM), pl.BlockSpec(memory_space=pltpu.SMEM)
    return pl.pallas_call(
        functools.partial(spectral_kernel, scale=scale, classes=classes, tokens=len(after)),
        in_specs=[smem, smem, vmem, vmem, pl.BlockSpec(memory_space=pltpu.HBM)] + [ANY] * len(after),
        out_specs=[vmem] * len(classes),
        scratch_shapes=[pltpu.VMEM((ncode, depth, 2 * width), jnp.bfloat16) for depth in depths]
        + [pltpu.VMEM((SLOTS, rows, mdev, samples), jnp.float32), pltpu.SemaphoreType.DMA((SLOTS,))],
        out_shape=[jax.ShapeDtypeStruct((edev // rows, width, rows, mdev), jnp.float32)] * len(classes),
        compiler_params=pltpu.CompilerParams(vmem_limit_bytes=VMEM_LIMIT),
        cost_estimate=pl.CostEstimate(
            flops=edev * mdev * 2 * sum(depths) * 2 * width * 2,
            bytes_accessed=traces.size * 4 + len(classes) * width * edev * mdev * 4, transcendentals=0,
        ),
        name="spectral",
    )(base, code_of, codes, table, traces, *after)


def steer_kernel(target_ref, spectra_ref, steer_hbm, *refs, cls, tokens):
    sent_ref, kept_ref, steer_ref, sems = refs[tokens:]
    slots, nb, mdev, width = steer_ref.shape
    count, _, edev, _ = sent_ref.shape
    half = width // 2

    def fetch(place, slot):
        source = steer_hbm.at[pl.ds(target_ref[place] * nb, nb), cls]
        return pltpu.make_async_copy(source, steer_ref.at[slot], sems.at[slot])

    for place in range(min(slots, 2 * count)):
        fetch(place, place).start()

    def complex_rows(w):
        return jnp.concatenate([w, jnp.concatenate([-w[:, half:], w[:, :half]], axis=1)], axis=0)

    def run(out_ref, first):
        def body(block, carry):
            place = first + block
            slot = lax.rem(place, slots)
            fetch(place, slot).wait()
            start = target_ref[place] * nb
            for i in range(nb):
                wh, wl = split(steer_ref[slot, i])
                parts = [spectra_ref[:, q, start + i].reshape(edev, mdev) for q in (0, 1)]
                sh, sl = split(jnp.concatenate(parts, axis=1))
                both = dot(jnp.concatenate([sh, sl], axis=0), complex_rows(wh))
                out_ref[block, i] = both[:edev] + both[edev:] + dot(sh, complex_rows(wl))

            @pl.when(place + slots < 2 * count)
            def _():
                fetch(place + slots, slot).start()

            return carry

        lax.fori_loop(0, count, body, 0)

    run(sent_ref, 0)
    run(kept_ref, count)


def steer_blocks(targets, spectra, steer, cls, after):
    count = targets.shape[0] // 2
    _, _, total, _, mdev = spectra.shape
    edev = spectra.shape[0] * spectra.shape[3]
    nb = total // (2 * count)
    width = steer.shape[3]
    shape = jax.ShapeDtypeStruct((count, nb, edev, width), jnp.float32)
    vmem, smem = pl.BlockSpec(memory_space=pltpu.VMEM), pl.BlockSpec(memory_space=pltpu.SMEM)
    return pl.pallas_call(
        functools.partial(steer_kernel, cls=cls, tokens=len(after)),
        in_specs=[smem, vmem, pl.BlockSpec(memory_space=pltpu.HBM)] + [ANY] * len(after),
        out_specs=[vmem, vmem],
        scratch_shapes=[pltpu.VMEM((4, nb, mdev, width), jnp.float32), pltpu.SemaphoreType.DMA((4,))],
        out_shape=[shape, shape],
        compiler_params=pltpu.CompilerParams(vmem_limit_bytes=STEER_VMEM_LIMIT),
        cost_estimate=pl.CostEstimate(
            flops=total * edev * 2 * mdev * width * 2 * 3,
            bytes_accessed=4 * total * (2 * edev * mdev + mdev * width + edev * width), transcendentals=0,
        ),
        name="steer",
    )(targets, spectra, steer, *after)


def decode_kernel(signs_ref, own_ref, near_ref, *refs, tokens):
    outs = refs[tokens:]
    nb = own_ref.shape[0]
    count, kdev, _ = signs_ref.shape
    signs = signs_ref[...].reshape(count * kdev, signs_ref.shape[2])
    for i in range(nb):
        high, low = split(jnp.concatenate([own_ref[i], near_ref[i]], axis=0))
        result = dot(signs, high) + dot(signs, low)
        for j in range(count):
            outs[j][i] = result[j * kdev : (j + 1) * kdev]


def decode(signs, own, near, after):
    nb, _, width = own.shape
    count, kdev, _ = signs.shape
    vmem = pl.BlockSpec(memory_space=pltpu.VMEM)
    return pl.pallas_call(
        functools.partial(decode_kernel, tokens=len(after)),
        in_specs=[vmem] * 3 + [ANY] * len(after),
        out_shape=[jax.ShapeDtypeStruct((nb, kdev, width), jnp.float32)] * count,
        compiler_params=pltpu.CompilerParams(vmem_limit_bytes=VMEM_LIMIT),
        cost_estimate=pl.CostEstimate(
            flops=signs.size * nb * width * 4, bytes_accessed=4 * (2 * own.size + count * nb * kdev * width), transcendentals=0
        ),
        name="decode",
    )(signs, own, near, *after)


def finish_kernel(*refs, scale, held):
    parts, out_ref = refs[held:-1], refs[-1]
    total = parts[0][...]
    for part in parts[1:]:
        total = total + part[...]
    out_ref[...] = total * scale


def finish(beams, own, arrived, cls, scale):
    nb, kdev, width = own.shape
    block = pl.BlockSpec((nb, kdev, width), lambda i: (0, 0, 0))
    held = [] if beams is None else [beams]
    return pl.pallas_call(
        functools.partial(finish_kernel, scale=scale, held=len(held)),
        grid=(1,),
        in_specs=[ANY] * len(held) + [block] * (1 + len(arrived)),
        out_specs=pl.BlockSpec((nb, None, kdev, width), lambda i: (0, cls, 0, 0)),
        out_shape=jax.ShapeDtypeStruct((nb, 4, kdev, width), jnp.float32),
        input_output_aliases={0: 0} if held else {},
        compiler_params=pltpu.CompilerParams(vmem_limit_bytes=VMEM_LIMIT),
        cost_estimate=pl.CostEstimate(
            flops=2 * nb * kdev * width, bytes_accessed=4 * (2 + len(arrived)) * nb * kdev * width, transcendentals=0
        ),
        name="finish",
    )(*held, own, *arrived)


def per_device(traces, codes, code_of, order, steer):
    edev, mdev, samples = traces.shape
    emissions = order.shape[0]
    bins = steer.shape[0]
    ne, nm = lax.axis_size("emit"), lax.axis_size("elem")
    me = lax.axis_index("elem")
    here = lax.axis_index("emit")
    base = (here * edev).reshape(1).astype(jnp.int32)
    steer = steer.reshape(bins // 4, 4, *steer.shape[1:])

    nbit = nm.bit_length() - 1
    upper = list(range(1, nbit))
    orders = (upper, upper[::-1])
    nrel = 1 << (nbit - 1)

    def mask_of(core, rel):
        return sum((rel >> (nbit - 2 - s) & 1) << bit for s, bit in enumerate(orders[core]))

    masks = np.array([[mask_of(core, nrel - 1 - p) for p in range(nrel)] for core in (0, 1)], np.int32)
    masks = np.stack([np.concatenate([1 ^ masks[1 - core], masks[core]]) for core in (0, 1)])
    targets = me ^ jnp.where(me & 1 == 0, masks[0], masks[1])
    swaps = [[(i, i ^ 1) for i in range(nm)]]
    for s in range(nbit - 1):
        swaps.append([(i, i ^ (1 << orders[i & 1][s])) for i in range(nm)])

    def signs_of(gap):
        rows = jnp.concatenate([lax.dynamic_slice_in_dim(order, z * edev, edev) for z in (here, here ^ gap)])
        others = others_of(gap, ne)
        wanted = jnp.stack([here ^ z for z in others + [0]])
        columns = wanted[:, None] * edev + jnp.arange(edev, dtype=jnp.int32)[None, :]
        parity = lax.population_count(columns[:, :, None] & rows[None, None, :]) & 1
        return others, (1 - 2 * parity).astype(jnp.bfloat16)

    scale = float(np.float32(1.0) / np.sqrt(np.float32(samples)))
    shrink = float(1.0 / np.sqrt(np.float32(emissions)))
    gaps = {cls: gap_of(cls, ne) for cls in range(4)}
    signs = {gap: signs_of(gap) for gap in sorted(set(gaps.values()))}

    last = []
    state = {cls: {} for cls in range(4)}
    beams = None

    def spectral(*classes):
        nonlocal last
        out = spectra_of(traces, codes, code_of, base, classes, bins, scale, last)
        for cls, spectra in zip(classes, out):
            state[cls]["spectra"] = spectra.reshape(edev // ROWS, 2, bins // 4, ROWS, mdev)
        last = [out[0]]

    def steered(cls):
        nonlocal last
        sent, kept = steer_blocks(targets, state[cls]["spectra"], steer, cls, last)
        last = [sent]
        state[cls]["kept"] = kept
        state[cls]["arrived"] = [lax.ppermute(sent, "elem", swaps[0])]

    def added(cls):
        nonlocal last
        kept, arrived = state[cls]["kept"], state[cls]["arrived"]
        stage = len(arrived)
        high = nrel >> (stage - 1)
        low = high >> 1
        kept, _ = lax.optimization_barrier((kept, last[0]))
        total = kept[nrel - high : nrel - low]
        for k, array in enumerate(arrived):
            start = (nrel >> k) - high
            total = total + array[start : start + high - low]
        last = [total]
        if stage < nbit:
            arrived.append(lax.ppermute(total, "elem", swaps[stage]))
        else:
            own = total[0]
            state[cls]["own"] = own
            state[cls]["near"] = lax.ppermute(own, "emit", [(z, z ^ gaps[cls]) for z in range(ne)])

    def decoded(cls):
        nonlocal last
        others, held = signs[gaps[cls]]
        out = decode(held, state[cls]["own"], state[cls]["near"], last)
        last = [out[0]]
        state[cls]["partial"] = out[-1]
        state[cls]["fetched"] = [
            lax.ppermute(part, "emit", [(z, z ^ gap) for z in range(ne)]) for part, gap in zip(out, others)
        ]

    def finished(cls):
        nonlocal beams
        beams = finish(beams, state[cls]["partial"], state[cls]["fetched"], cls, shrink)

    steps = {"spectral": spectral, "steer": steered, "sum": added, "decode": decoded, "finish": finished}
    for name, *values in plan(nbit):
        steps[name](*values)
    return beams.reshape(-1, *beams.shape[2:])


def plan(nbit):
    more = range(nbit - 2)
    return [
        ("spectral", 2, 0), ("steer", 2), ("steer", 0), ("sum", 2),
        ("spectral", 1), *(("sum", 2) for _ in more), ("steer", 1), ("sum", 2), ("sum", 0), ("sum", 1),
        ("spectral", 3), ("steer", 3), *(("sum", 0) for _ in more), *(("sum", 1) for _ in more), ("decode", 2),
        ("sum", 0), ("sum", 3), ("sum", 1), *(("sum", 3) for _ in more), ("decode", 1), ("sum", 3),
        ("decode", 3), ("decode", 0),
        ("finish", 2), ("finish", 1), ("finish", 0), ("finish", 3),
    ]


def gap_of(cls, ne):
    return ne // 2 if cls in (2, 0) else 1


def others_of(gap, ne):
    return [z for z in range(1, ne) if not z & gap]


def solution(mesh):
    placed = (P("emit", "elem", None), P(), P(), P(), P(None, "elem", None))

    return jax.shard_map(per_device, mesh=mesh, in_specs=placed, out_specs=P("elem", "emit", None), check_vma=False)
```
